512 devices in a mesh: dp: 8 (over y_hi, x), tile: 64 (over y_lo, z, core).
Axes of the slice: x: 4, y: 4 (y_hi: 2, y_lo: 2; y = y_hi * 2 + y_lo), z: 16, core: 2. Of those that a mesh axis runs over, the one named last changes fastest.
Arguments:
- ocean_state: bfloat16 [8, 256, 64, 768], P('dp', 'tile'), may hold values from -6 to 6
- cotangent: bfloat16 [8, 256, 64, 768], P('dp', 'tile'), may hold values from -6 to 6
- depth_kernel: float32 [7, 7, 768], replicated, may hold values from -0.875 to 0.875
- norm_gain: float32 [768], replicated, may hold values from 0.5 to 2
- expand_weight: bfloat16 [768, 3072], P('tile'), may hold values from -0.21875 to 0.21875
- expand_bias: float32 [3072], replicated, may hold values from -4 to 4
- reduce_weight: bfloat16 [3072, 768], P('tile'), may hold values from -0.109375 to 0.109375
- tile_slot: int32 [256], P('tile'), may hold values from -1 to 5, as said below
Outputs:
- state_grad: bfloat16 [8, 256, 64, 768], P('dp', 'tile')
- kernel_grad: float32 [7, 7, 768], replicated
- gain_grad: float32 [768], replicated
- bias_grad: float32 [3072], replicated
The draws below stay inside these ranges and needn't reach their ends.
Inputs may be any that keep to these rules, and one draw needn't show every extreme that they name: `tile_slot`: entry t is -1 for a land tile, k < 3 for slot k of the tile's own device, 3 + k for slot k of the device whose tile index differs by half of the axis; the tiles of a device and of that device together name each slot of either at most once, and on some pair of devices every slot is named.
All inputs are finite; a program needn't handle non-finite values.
Results may differ from the reference program's by a relative error of at most 0.0085.
Values may be sent and summed in bfloat16 or wider, within the bound.
No kernel may reach another device: no remote copies, remote signals or barrier semaphores. Data moves between devices by JAX's collectives and lax.ppermute only.
A program may use at most 64 MiB of HBM per device.

```python
import math
import jax
import jax.numpy as jnp
from jax import lax

C = 768
F = 3072
KS = 7
COLS = 64
TPD = 4
CAP = 3
TILE_ROWS = 1
NR = 256
SAMPLES = 8
N_TILE = 64


def draw_tile_slot(key, part):
    pair_count = N_TILE // 2
    subkeys = jax.random.split(key, 5)
    totals = jax.random.randint(subkeys[0], (pair_count,), 2, 2 * CAP + 1)
    lowest = jnp.maximum(0, totals - TPD)
    highest = jnp.minimum(TPD, totals)
    raw_pick = jax.random.randint(subkeys[1], (pair_count,), 0, 1 << 20)
    heavy_count = lowest + raw_pick % (highest - lowest + 1)
    forced = jax.random.randint(subkeys[2], (), 0, pair_count)
    is_forced = jnp.arange(pair_count) == forced
    totals = jnp.where(is_forced, 2 * CAP, totals)
    heavy_count = jnp.where(is_forced, TPD, heavy_count)
    light_count = totals - heavy_count
    swapped = jax.random.randint(subkeys[3], (pair_count,), 0, 2) == 1
    lower_count = jnp.where(swapped, light_count, heavy_count)
    upper_count = jnp.where(swapped, heavy_count, light_count)
    counts = jnp.concatenate([lower_count, upper_count])
    partner_counts = jnp.concatenate([upper_count, lower_count])
    tile_ranks = jax.vmap(lambda subkey: jax.random.permutation(subkey, TPD))(jax.random.split(subkeys[4], N_TILE))
    is_ocean = tile_ranks < counts[:, None]
    ocean_order = jnp.cumsum(is_ocean.astype(jnp.int32), axis=1) - 1
    slot_codes = jnp.where(ocean_order < CAP, ocean_order, partner_counts[:, None] + ocean_order)
    slot_codes = jnp.where(is_ocean, slot_codes, -1)
    return slot_codes.reshape(-1).astype(jnp.int32)


def levels(rng, dims, cuts, least, top_value):
    factor_of = 1.0
    for position, blocks in cuts:
        heights = jax.random.uniform(jax.random.fold_in(jax.random.fold_in(rng, 6), position), (blocks,), jnp.float32, least / len(cuts), top_value / len(cuts))
        factor_of = factor_of * jnp.repeat(jnp.exp(heights), dims[position] // blocks).reshape((-1,) + (1,) * (len(dims) - 1 - position))
    return factor_of


def scatter_about(key, dims, width, limit, shards=(), dtype=jnp.bfloat16):
    drawn = width * jax.random.normal(key, dims, jnp.float32)
    if shards:
        drawn = drawn * levels(key, dims, shards, -0.22, 0.18)
    return jnp.clip(drawn, -limit, limit).astype(dtype)


def setup_inputs(seed: int = 0) -> dict:
    key_list = jax.random.split(jax.random.key(seed), 9)
    ocean_state = scatter_about(key_list[0], (SAMPLES, NR, COLS, C), 1.0, 6.0, ((0, 8), (1, 64)))
    cotangent = scatter_about(key_list[1], (SAMPLES, NR, COLS, C), 1.0, 6.0, ((0, 8), (1, 64)))
    depth_kernel = scatter_about(key_list[2], (KS, KS, C), (KS * KS) ** -0.5, 0.875, (), jnp.float32)
    norm_gain = jnp.clip(jnp.exp(jax.random.uniform(key_list[3], (C,), jnp.float32, math.log(0.5), math.log(2.0))), 0.5, 2.0)
    expand_weight = scatter_about(key_list[4], (C, F), C ** -0.5, 0.21875, ((0, 64),))
    expand_bias = scatter_about(key_list[5], (F,), 1.0, 4.0, (), jnp.float32)
    reduce_weight = scatter_about(key_list[6], (F, C), F ** -0.5, 0.109375, ((0, 64),))
    tile_slot = draw_tile_slot(jax.random.fold_in(key_list[8], 71), 0)
    return dict(ocean_state=ocean_state, cotangent=cotangent, depth_kernel=depth_kernel, norm_gain=norm_gain, expand_weight=expand_weight, expand_bias=expand_bias, reduce_weight=reduce_weight, tile_slot=tile_slot)


def depthwise(padded, kernel, row_count, col_count):
    total = jnp.zeros(padded.shape[:-3] + (row_count, col_count, padded.shape[-1]), jnp.float32)
    for shift_row in range(KS):
        for shift_col in range(KS):
            total = total + kernel[shift_row, shift_col] * padded[..., shift_row:shift_row + row_count, shift_col:shift_col + col_count, :].astype(jnp.float32)
    return total

def gelu_slope(value):
    factor = math.sqrt(2.0 / math.pi)
    inner = factor * (value + 0.044715 * value * value * value)
    tangent = jnp.tanh(inner)
    return 0.5 * (1.0 + tangent) + 0.5 * value * (1.0 - tangent * tangent) * factor * (1.0 + 3.0 * 0.044715 * value * value)

def pointwise(scaled, masked, expand_weight, expand_bias, reduce_weight):
    hidden = jnp.dot(scaled, expand_weight, preferred_element_type=jnp.float32) + expand_bias
    back_act = jnp.dot(masked, reduce_weight.T, preferred_element_type=jnp.float32)
    back_hidden = (back_act * gelu_slope(hidden)).astype(jnp.bfloat16)
    back_scaled = jnp.dot(back_hidden, expand_weight.T, preferred_element_type=jnp.float32).astype(jnp.bfloat16)
    return (back_scaled, lax.optimization_barrier(jnp.sum(back_hidden.astype(jnp.float32), axis=0)))

def reference(ocean_state, cotangent, depth_kernel, norm_gain, expand_weight, expand_bias, reduce_weight, tile_slot):
    row_mask = jnp.repeat(tile_slot >= 0, TILE_ROWS).astype(jnp.bfloat16)
    cell_total = NR * COLS
    block = math.gcd(cell_total, 4096)

    def one_sample(inputs):
        state, grad_out = inputs
        padded = jnp.pad(state, ((3, 3), (3, 3), (0, 0)))
        mixed = depthwise(padded, depth_kernel, NR, COLS)
        centred = mixed - lax.optimization_barrier(jnp.mean(mixed, axis=-1, keepdims=True))
        inverse = lax.rsqrt(lax.optimization_barrier(jnp.mean(centred * centred, axis=-1, keepdims=True)) + 1e-06)
        normed = centred * inverse
        scaled = (normed * norm_gain).astype(jnp.bfloat16)
        masked = grad_out * row_mask[:, None, None]

        def one_block(pieces):
            return pointwise(pieces[0], pieces[1], expand_weight, expand_bias, reduce_weight)
        block_scaled, block_bias = lax.map(one_block, (scaled.reshape(-1, block, C), masked.reshape(-1, block, C)))
        back_scaled = block_scaled.reshape(NR, COLS, C).astype(jnp.float32)
        gain_part = lax.optimization_barrier(jnp.sum(back_scaled * normed, axis=(0, 1)))
        back_norm = back_scaled * norm_gain
        back_mixed = inverse * (back_norm - lax.optimization_barrier(jnp.mean(back_norm, axis=-1, keepdims=True)) - normed * lax.optimization_barrier(jnp.mean(back_norm * normed, axis=-1, keepdims=True)))
        back_mixed = back_mixed.astype(jnp.bfloat16)
        back_float = back_mixed.astype(jnp.float32)
        kernel_rows = []
        for shift_row in range(KS):
            kernel_cols = []
            for shift_col in range(KS):
                window = padded[shift_row:shift_row + NR, shift_col:shift_col + COLS, :].astype(jnp.float32)
                kernel_cols.append(lax.optimization_barrier(jnp.sum(window * back_float, axis=(0, 1))))
            kernel_rows.append(jnp.stack(kernel_cols))
        kernel_part = jnp.stack(kernel_rows)
        back_padded = jnp.pad(back_mixed, ((3, 3), (3, 3), (0, 0)))
        through = depthwise(back_padded, depth_kernel[::-1, ::-1], NR, COLS)
        state_grad = (grad_out.astype(jnp.float32) + through).astype(jnp.bfloat16)
        return (state_grad, kernel_part, gain_part, lax.optimization_barrier(jnp.sum(block_bias, axis=0)))
    state_grad, kernel_parts, gain_parts, bias_parts = lax.map(one_sample, (ocean_state, cotangent))
    return (state_grad, lax.optimization_barrier(jnp.sum(kernel_parts, axis=0)), lax.optimization_barrier(jnp.sum(gain_parts, axis=0)), lax.optimization_barrier(jnp.sum(bias_parts, axis=0)))
```

```python
import math

import jax
import jax.numpy as jnp
from jax import lax
from jax.experimental import pallas as pl
from jax.experimental.pallas import tpu as pltpu
from jax.sharding import Mesh
from jax.sharding import PartitionSpec as P

KS = 7
TILE = ("yl", "z", "c")
DP = ("yh", "x")
PLANE = ("yh", "x", "yl", "c")


def with_halo(cells, width):
    count = lax.axis_size(TILE)
    ends = count - 1
    head = lax.slice_in_dim(cells, 0, width, axis=1)
    tail = lax.slice_in_dim(cells, cells.shape[1] - width, cells.shape[1], axis=1)
    return jnp.concatenate(
        [
            lax.ppermute(tail, TILE, [(i, i + 1) for i in range(ends)]),
            cells,
            lax.ppermute(head, TILE, [(i + 1, i) for i in range(ends)]),
        ],
        axis=1,
    )


def depthwise(padded, kernel, row_count, col_count):
    total = None
    for shift_row in range(KS):
        band = padded[..., shift_row : shift_row + row_count, :, :]
        part = kernel[shift_row, 0] * band[..., 0:col_count, :].astype(jnp.float32)
        for shift_col in range(1, KS):
            part = part + kernel[shift_row, shift_col] * band[
                ..., shift_col : shift_col + col_count, :
            ].astype(jnp.float32)
        total = part if total is None else total + part
    return total


def gelu_slope(value):
    factor = math.sqrt(2.0 / math.pi)
    inner = factor * (value + 0.044715 * value * value * value)
    tangent = jnp.tanh(inner)
    return 0.5 * (1.0 + tangent) + 0.5 * value * (1.0 - tangent * tangent) * factor * (
        1.0 + 3.0 * 0.044715 * value * value
    )


def sum_everywhere(parts):
    lanes = 128
    plane = lax.axis_size(PLANE)
    depth = lax.axis_size("z")
    rows = [part.reshape(-1, lanes) for part in parts]
    used = sum(piece.shape[0] for piece in rows)
    share = -(-used // (8 * plane)) * 8
    rows.append(jnp.zeros((share * plane - used, lanes), jnp.float32))
    stacked = jnp.concatenate(rows).reshape(plane, share, lanes)
    mine = jnp.sum(lax.all_to_all(stacked, PLANE, 0, 0), axis=0)
    mine = jnp.broadcast_to(mine[None], (depth, share, lanes))
    mine = jnp.sum(lax.all_to_all(mine, "z", 0, 0), axis=0)
    mine = jnp.broadcast_to(mine[None], (plane, share, lanes))
    full = lax.all_to_all(mine, PLANE, 0, 0).reshape(plane * share, lanes)
    out, start = [], 0
    for part in parts:
        count = part.size // lanes
        out.append(full[start : start + count].reshape(part.shape))
        start += count
    return out


NEAR = ((0, 1), (1, 0), (2, 3), (3, 2))
FAR = ((0, 3), (3, 0), (1, 2), (2, 1))
HIGH, WIDE = 24, 384


def column_of_weights(expand_weight, reduce_weight):
    core, column = lax.axis_index("c"), lax.axis_index("x")
    pair, side = column // 2, column % 2
    thin, units = expand_weight.shape
    part = lax.dynamic_slice(expand_weight, (0, side * (units // 2)), (thin, units // 2))
    row = lax.broadcasted_iota(jnp.int32, (units // 2, 2 * WIDE), 0)
    col = lax.broadcasted_iota(jnp.int32, (units // 2, 2 * WIDE), 1)
    band = col // WIDE * 2 + pair
    at = col % WIDE
    pick = row == at // HIGH * (4 * HIGH) + at % HIGH + band * HIGH
    chosen = jnp.dot(part, pick.astype(jnp.bfloat16), preferred_element_type=jnp.float32)
    both = lax.all_gather(chosen.astype(jnp.bfloat16), "c", axis=0)
    piece = jnp.where(
        lax.axis_index("yh") == 0,
        lax.dynamic_slice(both, (0, 0, core * WIDE), (2, thin, WIDE)).reshape(HIGH, WIDE),
        lax.dynamic_slice(reduce_weight, (pair * HIGH, side * WIDE), (HIGH, WIDE)),
    )
    depth = lax.axis_size("z")
    return lax.all_to_all(jnp.broadcast_to(piece[None], (depth, HIGH, WIDE)), "z", 0, 0)


def sheets_of_weights(column):
    depth = column.shape[0]
    own = lax.all_to_all(
        jnp.broadcast_to(column[None], (4, depth, HIGH, WIDE)), ("yh", "yl"), 0, 0
    ).reshape(2, 2 * depth * HIGH, WIDE)
    own_expand, own_reduce = own[0], own[1]
    near_expand = lax.ppermute(own_expand, "x", NEAR)
    far_reduce = lax.ppermute(own_reduce, "x", FAR)
    near_reduce = lax.ppermute(own_reduce, "x", NEAR)
    far_expand = lax.ppermute(own_expand, "x", FAR)
    across_expand = lax.ppermute(near_expand, "x", FAR)
    across_reduce = lax.ppermute(far_reduce, "x", NEAR)
    return (own_expand, near_expand, own_reduce, near_reduce), (
        far_expand,
        across_expand,
        far_reduce,
        across_reduce,
    )


def add_band(band, first_side, scaled_ref, masked_ref, bias_ref, sheets, bias_out, expand, reduce, sem, total):
    wide = expand.shape[2]
    contract_last = (((1,), (1,)), ((), ()))
    copies = [
        pltpu.make_async_copy(sheets[0], expand.at[0], sem.at[0]),
        pltpu.make_async_copy(sheets[2], reduce.at[0], sem.at[2]),
        pltpu.make_async_copy(sheets[3], reduce.at[1], sem.at[3]),
        pltpu.make_async_copy(sheets[1], expand.at[1], sem.at[1]),
    ]
    for copy in copies:
        copy.start()
    sides = (first_side, 1 - first_side)
    for part in range(2):
        half = pl.ds(pl.multiple_of(sides[part] * wide, wide), wide)
        copies[3 if part else 0].wait()
        hidden = jnp.dot(scaled_ref[...], expand[part], preferred_element_type=jnp.float32)
        slope = gelu_slope(hidden + bias_ref[band * 2 + sides[part]])
        back_act = None
        for other in range(2):
            if part == 0:
                copies[1 + other].wait()
            term = lax.dot_general(
                masked_ref[:, pl.ds(pl.multiple_of(sides[other] * wide, wide), wide)],
                reduce[other, half, :],
                contract_last,
                preferred_element_type=jnp.float32,
            )
            back_act = term if back_act is None else back_act + term
        back_hidden = (back_act * slope).astype(jnp.bfloat16)
        bias_out[band * 2 + sides[part]] = jnp.sum(back_hidden.astype(jnp.float32), axis=0, keepdims=True)
        total[...] += lax.dot_general(
            back_hidden, expand[part], contract_last, preferred_element_type=jnp.float32
        )


def first_body(
    where_ref, scaled_ref, masked_ref, bias_ref, s0, s1, s2, s3, total_ref, bias_out, expand, reduce, sem
):
    column, core = where_ref[0], where_ref[1]
    bias_out[...] = jnp.zeros_like(bias_out)
    total_ref[...] = jnp.zeros_like(total_ref)
    add_band(
        2 * core + lax.div(column, 2), lax.rem(column, 2), scaled_ref, masked_ref, bias_ref,
        (s0, s1, s2, s3), bias_out, expand, reduce, sem, total_ref,
    )


def second_body(
    where_ref, scaled_ref, masked_ref, bias_ref, s0, s1, s2, s3, sum_ref, bias_in,
    mine_ref, other_ref, bias_out, expand, reduce, total, sem,
):
    column, core = where_ref[0], where_ref[1]
    cells = mine_ref.shape[0]
    bias_out[...] = bias_in[...]
    total[...] = sum_ref[...]
    add_band(
        2 * core + 1 - lax.div(column, 2), 1 - lax.rem(column, 2), scaled_ref, masked_ref, bias_ref,
        (s0, s1, s2, s3), bias_out, expand, reduce, sem, total,
    )
    mine_ref[...] = total[pl.ds(pl.multiple_of(core * cells, cells), cells), :]
    other_ref[...] = total[pl.ds(pl.multiple_of((1 - core) * cells, cells), cells), :]


def norm_body(mine_ref, other_ref, normed_ref, inverse_ref, gain_ref, mixed_ref, gain_part_ref):
    gain_part_ref[...] = jnp.zeros_like(gain_part_ref)
    rows = 32

    def finish(step, carry):
        at = pl.ds(pl.multiple_of(step * rows, rows), rows)
        back = (mine_ref[at, :] + other_ref[at, :]).astype(jnp.bfloat16).astype(jnp.float32)
        normed = normed_ref[at, :]
        gain_part_ref[...] += jnp.sum(back * normed, axis=0, keepdims=True)
        back_norm = back * gain_ref[...]
        mixed = inverse_ref[at, :] * (
            back_norm
            - jnp.mean(back_norm, axis=-1, keepdims=True)
            - normed * jnp.mean(back_norm * normed, axis=-1, keepdims=True)
        )
        mixed_ref[at, :] = mixed.astype(jnp.bfloat16)
        return carry

    lax.fori_loop(0, mine_ref.shape[0] // rows, finish, 0)


def pointwise(where, scaled, masked, normed, inverse, gain, bias, first, second):
    cells, channels = normed.shape
    vmem = pl.BlockSpec(memory_space=pltpu.VMEM)
    there = pl.BlockSpec(memory_space=pl.ANY)
    smem = pl.BlockSpec(memory_space=pltpu.SMEM)
    weights = [pltpu.VMEM((2, channels, WIDE), jnp.bfloat16) for _ in range(2)]
    sem = pltpu.SemaphoreType.DMA((4,))
    whole = jax.ShapeDtypeStruct((2 * cells, channels), jnp.float32)
    half = jax.ShapeDtypeStruct((cells, channels), jnp.float32)
    bias_shape = jax.ShapeDtypeStruct(bias.shape, jnp.float32)
    params = pltpu.CompilerParams(vmem_limit_bytes=32 * 1024 * 1024)
    cost = pl.CostEstimate(
        flops=12 * cells * channels * channels, transcendentals=2 * cells * channels, bytes_accessed=20 * 1024 * 1024
    )
    total, bias_part = pl.pallas_call(
        first_body,
        out_shape=(whole, bias_shape),
        in_specs=[smem] + [vmem] * 3 + [there] * 4,
        out_specs=(vmem, vmem),
        scratch_shapes=weights + [sem],
        compiler_params=params,
        cost_estimate=cost,
        name="pointwise_first",
    )(where, scaled, masked, bias, *first)
    mine, other, bias_part = pl.pallas_call(
        second_body,
        out_shape=(half, half, bias_shape),
        in_specs=[smem] + [vmem] * 3 + [there] * 4 + [vmem] * 2,
        out_specs=(vmem, vmem, vmem),
        scratch_shapes=weights + [pltpu.VMEM((2 * cells, channels), jnp.float32), sem],
        compiler_params=params,
        cost_estimate=cost,
        name="pointwise_second",
    )(where, scaled, masked, bias, *second, total, bias_part)
    other = lax.ppermute(other, "c", ((0, 1), (1, 0)))
    mixed, gain_part = pl.pallas_call(
        norm_body,
        out_shape=(
            jax.ShapeDtypeStruct((cells, channels), jnp.bfloat16),
            jax.ShapeDtypeStruct((1, channels), jnp.float32),
        ),
        in_specs=[vmem] * 5,
        out_specs=(vmem, vmem),
        compiler_params=params,
        name="norm_back",
    )(mine, other, normed, inverse, gain)
    return mixed, gain_part, bias_part


def local(
    ocean_state,
    cotangent,
    depth_kernel,
    norm_gain,
    expand_weight,
    expand_bias,
    reduce_weight,
    tile_slot,
):
    samples, row_count, col_count, channels = ocean_state.shape
    tile_count = tile_slot.shape[0]
    tile_rows = row_count // tile_count
    rim = KS // 2
    weights_column = column_of_weights(expand_weight, reduce_weight)
    padded = with_halo(ocean_state, rim)
    padded = jnp.pad(padded, ((0, 0), (0, 0), (rim, rim), (0, 0)))
    mixed = depthwise(padded, depth_kernel, row_count, col_count)
    centred = mixed - jnp.mean(mixed, axis=-1, keepdims=True)
    inverse = lax.rsqrt(jnp.mean(centred * centred, axis=-1, keepdims=True) + 1e-06)
    normed = centred * inverse
    scaled = (normed * norm_gain).astype(jnp.bfloat16)
    row_mask = jnp.repeat(tile_slot >= 0, tile_rows).astype(jnp.bfloat16)
    masked = cotangent * row_mask[None, :, None, None]
    where = jnp.stack([lax.axis_index("x"), lax.axis_index("c")]).astype(jnp.int32)
    depth = lax.axis_size("z")
    ready = (
        scaled.reshape(-1, channels),
        masked.reshape(-1, channels),
        normed.reshape(-1, channels),
        inverse.reshape(-1, 1),
        norm_gain.reshape(1, channels),
        expand_bias.reshape(2, depth, 4, HIGH).transpose(2, 0, 1, 3).reshape(8, 1, WIDE),
        where,
    )
    weights_column, (scaled, masked, normed, inverse, gain, bias, where) = lax.optimization_barrier(
        (weights_column, ready)
    )
    first, second = sheets_of_weights(weights_column)
    scaled = lax.all_gather(scaled, "c", axis=0, tiled=True)
    masked = lax.all_gather(masked, "c", axis=0, tiled=True)
    back_mixed, gain_part, bias_part = pointwise(
        where, scaled, masked, normed, inverse, gain, bias, first, second
    )
    back_mixed = back_mixed.reshape(samples, row_count, col_count, channels)
    gain_part = gain_part.reshape(channels)
    bias_part = bias_part.reshape(-1)
    mixed_float = back_mixed.astype(jnp.float32)
    kernel_rows = []
    for shift_row in range(KS):
        band = padded[:, shift_row : shift_row + row_count, :, :]
        kernel_cols = [
            jnp.sum(
                band[:, :, shift_col : shift_col + col_count, :].astype(jnp.float32) * mixed_float,
                axis=(0, 1, 2),
            )
            for shift_col in range(KS)
        ]
        kernel_rows.append(jnp.stack(kernel_cols))
    kernel_part = jnp.stack(kernel_rows)
    back_padded = with_halo(back_mixed, rim)
    back_padded = jnp.pad(back_padded, ((0, 0), (0, 0), (rim, rim), (0, 0)))
    through = depthwise(back_padded, depth_kernel[::-1, ::-1], row_count, col_count)
    state_grad = (cotangent.astype(jnp.float32) + through).astype(jnp.bfloat16)
    kernel_grad, gain_grad, bias_grad = sum_everywhere((kernel_part, gain_part, bias_part))
    bias_grad = bias_grad.reshape(4, 2, depth, HIGH).transpose(1, 2, 0, 3).reshape(-1)
    return (state_grad, kernel_grad, gain_grad, bias_grad)


def solution(mesh):
    wide = Mesh(mesh.devices.reshape(2, 4, 2, 16, 2), ("yh", "x", "yl", "z", "c"))
    return jax.shard_map(
        local,
        mesh=wide,
        in_specs=(
            P(DP, TILE, None, None),
            P(DP, TILE, None, None),
            P(),
            P(),
            P(TILE, None),
            P(),
            P(TILE, None),
            P(TILE),
        ),
        out_specs=(P(DP, TILE, None, None), P(), P(), P()),
        check_vma=False,
    )
```

```python
import math

import jax
import jax.numpy as jnp
from jax import lax
from jax.experimental import pallas as pl
from jax.experimental.pallas import tpu as pltpu
from jax.sharding import Mesh
from jax.sharding import PartitionSpec as P

KS = 7
LANES = 128
TILE = ("yl", "z", "c")
DP = ("yh", "x")
PLANE = ("yh", "x", "yl", "c")


def exchange_rims(cells, width):
    count = lax.axis_size(TILE)
    ends = count - 1
    head = lax.slice_in_dim(cells, 0, width, axis=1)
    tail = lax.slice_in_dim(cells, cells.shape[1] - width, cells.shape[1], axis=1)
    return (
        lax.ppermute(tail, TILE, [(i, i + 1) for i in range(ends)]),
        lax.ppermute(head, TILE, [(i + 1, i) for i in range(ends)]),
    )


def join_rims(cells, rims, width):
    padded = jnp.concatenate([rims[0], cells, rims[1]], axis=1)
    return jnp.pad(padded, ((0, 0), (0, 0), (width, width), (0, 0)))


def depthwise(padded, kernel, row_count, col_count):
    total = None
    for shift_row in range(KS):
        band = padded[..., shift_row : shift_row + row_count, :, :]
        part = kernel[shift_row, 0] * band[..., 0:col_count, :].astype(jnp.float32)
        for shift_col in range(1, KS):
            part = part + kernel[shift_row, shift_col] * band[
                ..., shift_col : shift_col + col_count, :
            ].astype(jnp.float32)
        total = part if total is None else total + part
    return total


def gelu_slope(value):
    factor = math.sqrt(2.0 / math.pi)
    inner = factor * (value + 0.044715 * value * value * value)
    tangent = jnp.tanh(inner)
    return 0.5 * (1.0 + tangent) + 0.5 * value * (1.0 - tangent * tangent) * factor * (
        1.0 + 3.0 * 0.044715 * value * value
    )


def sum_shares(parts):
    plane = lax.axis_size(PLANE)
    depth = lax.axis_size("z")
    rows = [part.reshape(-1, LANES) for part in parts]
    used = sum(piece.shape[0] for piece in rows)
    share = -(-used // (8 * plane)) * 8
    rows.append(jnp.zeros((share * plane - used, LANES), jnp.float32))
    stacked = jnp.concatenate(rows).reshape(plane, share, LANES)
    mine = jnp.sum(lax.all_to_all(stacked, PLANE, 0, 0), axis=0)
    mine = jnp.broadcast_to(mine[None], (depth, share, LANES))
    return lax.all_to_all(mine, "z", 0, 0)


def gather_sums(shares, parts):
    plane = lax.axis_size(PLANE)
    mine = jnp.sum(shares, axis=0)
    full = lax.all_to_all(jnp.broadcast_to(mine[None], (plane, *mine.shape)), PLANE, 0, 0)
    full = full.reshape(-1, LANES)
    out, start = [], 0
    for part in parts:
        count = part.size // LANES
        out.append(full[start : start + count].reshape(part.shape))
        start += count
    return out


NEAR = ((0, 1), (1, 0), (2, 3), (3, 2))
FAR = ((0, 3), (3, 0), (1, 2), (2, 1))
HIGH, WIDE = 24, 384


def column_of_weights(expand_weight, reduce_weight):
    core, column = lax.axis_index("c"), lax.axis_index("x")
    pair, side = column // 2, column % 2
    thin, units = expand_weight.shape
    part = lax.dynamic_slice(expand_weight, (0, side * (units // 2)), (thin, units // 2))
    row = lax.broadcasted_iota(jnp.int32, (units // 2, 2 * WIDE), 0)
    col = lax.broadcasted_iota(jnp.int32, (units // 2, 2 * WIDE), 1)
    band = col // WIDE * 2 + pair
    at = col % WIDE
    pick = row == at // HIGH * (4 * HIGH) + at % HIGH + band * HIGH
    chosen = jnp.dot(part, pick.astype(jnp.bfloat16), preferred_element_type=jnp.float32)
    both = lax.all_gather(chosen.astype(jnp.bfloat16), "c", axis=0)
    piece = jnp.where(
        lax.axis_index("yh") == 0,
        lax.dynamic_slice(both, (0, 0, core * WIDE), (2, thin, WIDE)).reshape(HIGH, WIDE),
        lax.dynamic_slice(reduce_weight, (pair * HIGH, side * WIDE), (HIGH, WIDE)),
    )
    depth = lax.axis_size("z")
    return lax.all_to_all(jnp.broadcast_to(piece[None], (depth, HIGH, WIDE)), "z", 0, 0)


def sheets_of_weights(column, scaled, masked):
    depth = column.shape[0]
    own = lax.all_to_all(jnp.broadcast_to(column[None], (4, depth, HIGH, WIDE)), ("yh", "yl"), 0, 0)
    own = own.reshape(2, 2 * depth * HIGH, WIDE)
    own, scaled, masked = lax.optimization_barrier((own, scaled, masked))
    own_expand, own_reduce = own[0], own[1]
    near_expand = lax.ppermute(own_expand, "x", NEAR)
    far_reduce = lax.ppermute(own_reduce, "x", FAR)
    near_reduce = lax.ppermute(own_reduce, "x", NEAR)
    far_expand = lax.ppermute(own_expand, "x", FAR)
    across_expand = lax.ppermute(near_expand, "x", FAR)
    across_reduce = lax.ppermute(far_reduce, "x", NEAR)
    scaled = lax.all_gather(scaled, "c", axis=0, tiled=True)
    masked = lax.all_gather(masked, "c", axis=0, tiled=True)
    first = own_expand, near_expand, own_reduce, near_reduce
    second = far_expand, across_expand, far_reduce, across_reduce
    return first, second, scaled, masked


def add_band(band, first_side, scaled_ref, masked_ref, bias_ref, expand, reduce, bias_out, total):
    contract_last = (((1,), (1,)), ((), ()))
    sides = (first_side, 1 - first_side)
    for part in range(2):
        half = pl.ds(pl.multiple_of(sides[part] * WIDE, WIDE), WIDE)
        hidden = jnp.dot(scaled_ref[...], expand[part][...], preferred_element_type=jnp.float32)
        slope = gelu_slope(hidden + bias_ref[band * 2 + sides[part]])
        back_act = None
        for other in range(2):
            term = lax.dot_general(
                masked_ref[:, pl.ds(pl.multiple_of(sides[other] * WIDE, WIDE), WIDE)],
                reduce[other][half, :],
                contract_last,
                preferred_element_type=jnp.float32,
            )
            back_act = term if back_act is None else back_act + term
        back_hidden = (back_act * slope).astype(jnp.bfloat16)
        bias_out[band * 2 + sides[part]] = jnp.sum(back_hidden.astype(jnp.float32), axis=0, keepdims=True)
        total[...] += lax.dot_general(
            back_hidden, expand[part][...], contract_last, preferred_element_type=jnp.float32
        )


def first_body(where_ref, scaled_ref, masked_ref, bias_ref, e0, e1, r0, r1, total_ref, bias_out):
    column, core = where_ref[0], where_ref[1]
    bias_out[...] = jnp.zeros_like(bias_out)
    total_ref[...] = jnp.zeros_like(total_ref)
    add_band(
        2 * core + lax.div(column, 2), lax.rem(column, 2), scaled_ref, masked_ref, bias_ref,
        (e0, e1), (r0, r1), bias_out, total_ref,
    )


def second_body(
    where_ref, scaled_ref, masked_ref, bias_ref, e0, e1, r0, r1, sum_ref, bias_in,
    mine_ref, other_ref, bias_out, total,
):
    column, core = where_ref[0], where_ref[1]
    cells = mine_ref.shape[0]
    bias_out[...] = bias_in[...]
    total[...] = sum_ref[...]
    add_band(
        2 * core + 1 - lax.div(column, 2), 1 - lax.rem(column, 2), scaled_ref, masked_ref, bias_ref,
        (e0, e1), (r0, r1), bias_out, total,
    )
    mine_ref[...] = total[pl.ds(pl.multiple_of(core * cells, cells), cells), :]
    other_ref[...] = total[pl.ds(pl.multiple_of((1 - core) * cells, cells), cells), :]


def norm_body(mine_ref, other_ref, normed_ref, inverse_ref, gain_ref, mixed_ref, gain_part_ref):
    gain_part_ref[...] = jnp.zeros_like(gain_part_ref)
    rows = 32

    def finish(step, carry):
        at = pl.ds(pl.multiple_of(step * rows, rows), rows)
        back = (mine_ref[at, :] + other_ref[at, :]).astype(jnp.bfloat16).astype(jnp.float32)
        normed = normed_ref[at, :]
        gain_part_ref[...] += jnp.sum(back * normed, axis=0, keepdims=True)
        back_norm = back * gain_ref[...]
        mixed = inverse_ref[at, :] * (
            back_norm
            - jnp.mean(back_norm, axis=-1, keepdims=True)
            - normed * jnp.mean(back_norm * normed, axis=-1, keepdims=True)
        )
        mixed_ref[at, :] = mixed.astype(jnp.bfloat16)
        return carry

    lax.fori_loop(0, mine_ref.shape[0] // rows, finish, 0)


def pointwise(where, scaled, masked, normed, inverse, gain, bias, first, second):
    cells, channels = normed.shape
    vmem = pl.BlockSpec(memory_space=pltpu.VMEM)
    smem = pl.BlockSpec(memory_space=pltpu.SMEM)
    whole = jax.ShapeDtypeStruct((2 * cells, channels), jnp.float32)
    half = jax.ShapeDtypeStruct((cells, channels), jnp.float32)
    bias_shape = jax.ShapeDtypeStruct(bias.shape, jnp.float32)
    params = pltpu.CompilerParams(vmem_limit_bytes=32 * 1024 * 1024)
    cost = pl.CostEstimate(
        flops=12 * cells * channels * channels, transcendentals=2 * cells * channels, bytes_accessed=20 * 1024 * 1024
    )
    total, bias_part = pl.pallas_call(
        first_body,
        out_shape=(whole, bias_shape),
        in_specs=[smem] + [vmem] * 7,
        out_specs=(vmem, vmem),
        compiler_params=params,
        cost_estimate=cost,
        name="pointwise_first",
    )(where, scaled, masked, bias, *first)
    mine, other, bias_part = pl.pallas_call(
        second_body,
        out_shape=(half, half, bias_shape),
        in_specs=[smem] + [vmem] * 9,
        out_specs=(vmem, vmem, vmem),
        scratch_shapes=[pltpu.VMEM((2 * cells, channels), jnp.float32)],
        compiler_params=params,
        cost_estimate=cost,
        name="pointwise_second",
    )(where, scaled, masked, bias, *second, total, bias_part)
    other = lax.ppermute(other, "c", ((0, 1), (1, 0)))
    mixed, gain_part = pl.pallas_call(
        norm_body,
        out_shape=(
            jax.ShapeDtypeStruct((cells, channels), jnp.bfloat16),
            jax.ShapeDtypeStruct((1, channels), jnp.float32),
        ),
        in_specs=[vmem] * 5,
        out_specs=(vmem, vmem),
        compiler_params=params,
        name="norm_back",
    )(mine, other, normed, inverse, gain)
    return mixed, gain_part, bias_part


def local(
    ocean_state,
    cotangent,
    depth_kernel,
    norm_gain,
    expand_weight,
    expand_bias,
    reduce_weight,
    tile_slot,
):
    samples, row_count, col_count, channels = ocean_state.shape
    tile_count = tile_slot.shape[0]
    tile_rows = row_count // tile_count
    rim = KS // 2
    weights_column = column_of_weights(expand_weight, reduce_weight)
    rims = exchange_rims(ocean_state, rim)
    padded = join_rims(ocean_state, rims, rim)
    mixed = depthwise(padded, depth_kernel, row_count, col_count)
    centred = mixed - jnp.mean(mixed, axis=-1, keepdims=True)
    inverse = lax.rsqrt(jnp.mean(centred * centred, axis=-1, keepdims=True) + 1e-06)
    normed = centred * inverse
    scaled = (normed * norm_gain).astype(jnp.bfloat16)
    row_mask = jnp.repeat(tile_slot >= 0, tile_rows).astype(jnp.bfloat16)
    masked = cotangent * row_mask[None, :, None, None]
    where = jnp.stack([lax.axis_index("x"), lax.axis_index("c")]).astype(jnp.int32)
    depth = lax.axis_size("z")
    ready = (
        scaled.reshape(-1, channels),
        masked.reshape(-1, channels),
        normed.reshape(-1, channels),
        inverse.reshape(-1, 1),
        norm_gain.reshape(1, channels),
        expand_bias.reshape(2, depth, 4, HIGH).transpose(2, 0, 1, 3).reshape(8, 1, WIDE),
        where,
    )
    scaled, masked, normed, inverse, gain, bias, where = ready
    first, second, scaled, masked = sheets_of_weights(weights_column, scaled, masked)
    back_mixed, gain_part, bias_part = pointwise(
        where, scaled, masked, normed, inverse, gain, bias, first, second
    )
    back_mixed = back_mixed.reshape(samples, row_count, col_count, channels)
    gain_part = gain_part.reshape(channels)
    bias_part = bias_part.reshape(-1)
    mixed_float = back_mixed.astype(jnp.float32)
    kernel_rows = []
    for shift_row in range(KS):
        band = padded[:, shift_row : shift_row + row_count, :, :]
        kernel_cols = [
            jnp.sum(
                band[:, :, shift_col : shift_col + col_count, :].astype(jnp.float32) * mixed_float,
                axis=(0, 1, 2),
            )
            for shift_col in range(KS)
        ]
        kernel_rows.append(jnp.stack(kernel_cols))
    kernel_part = jnp.stack(kernel_rows)
    rims = exchange_rims(back_mixed, rim)
    parts = kernel_part, gain_part, bias_part
    shares = sum_shares(parts)
    back_padded = join_rims(back_mixed, rims, rim)
    through = depthwise(back_padded, depth_kernel[::-1, ::-1], row_count, col_count)
    state_grad = (cotangent.astype(jnp.float32) + through).astype(jnp.bfloat16)
    kernel_grad, gain_grad, bias_grad = gather_sums(shares, parts)
    bias_grad = bias_grad.reshape(4, 2, depth, HIGH).transpose(1, 2, 0, 3).reshape(-1)
    return (state_grad, kernel_grad, gain_grad, bias_grad)


def solution(mesh):
    wide = Mesh(mesh.devices.reshape(2, 4, 2, 16, 2), ("yh", "x", "yl", "z", "c"))
    return jax.shard_map(
        local,
        mesh=wide,
        in_specs=(
            P(DP, TILE, None, None),
            P(DP, TILE, None, None),
            P(),
            P(),
            P(TILE, None),
            P(),
            P(TILE, None),
            P(TILE),
        ),
        out_specs=(P(DP, TILE, None, None), P(), P(), P()),
        check_vma=False,
    )
```

```python
import math

import jax
import jax.numpy as jnp
from jax import lax
from jax.experimental import pallas as pl
from jax.experimental.pallas import tpu as pltpu
from jax.sharding import Mesh
from jax.sharding import PartitionSpec as P

KS = 7
LANES = 128
TILE = ("yl", "z", "c")
DP = ("yh", "x")
PLANE = ("yh", "x", "yl", "c")


def exchange_rims(cells, width):
    count = lax.axis_size(TILE)
    ends = count - 1
    head = lax.slice_in_dim(cells, 0, width, axis=1)
    tail = lax.slice_in_dim(cells, cells.shape[1] - width, cells.shape[1], axis=1)
    return (
        lax.ppermute(tail, TILE, [(i, i + 1) for i in range(ends)]),
        lax.ppermute(head, TILE, [(i + 1, i) for i in range(ends)]),
    )


def join_rims(cells, rims, width):
    padded = jnp.concatenate([rims[0], cells, rims[1]], axis=1)
    return jnp.pad(padded, ((0, 0), (0, 0), (width, width), (0, 0)))


def depthwise(padded, kernel, row_count, col_count):
    total = None
    for shift_row in range(KS):
        band = padded[..., shift_row : shift_row + row_count, :, :]
        part = kernel[shift_row, 0] * band[..., 0:col_count, :].astype(jnp.float32)
        for shift_col in range(1, KS):
            part = part + kernel[shift_row, shift_col] * band[
                ..., shift_col : shift_col + col_count, :
            ].astype(jnp.float32)
        total = part if total is None else total + part
    return total


def gelu_slope(value):
    factor = math.sqrt(2.0 / math.pi)
    inner = factor * (value + 0.044715 * value * value * value)
    tangent = jnp.tanh(inner)
    return 0.5 * (1.0 + tangent) + 0.5 * value * (1.0 - tangent * tangent) * factor * (
        1.0 + 3.0 * 0.044715 * value * value
    )


def sum_shares(parts):
    plane = lax.axis_size(PLANE)
    depth = lax.axis_size("z")
    rows = [part.reshape(-1, LANES) for part in parts]
    used = sum(piece.shape[0] for piece in rows)
    share = -(-used // (8 * plane)) * 8
    rows.append(jnp.zeros((share * plane - used, LANES), jnp.float32))
    stacked = jnp.concatenate(rows).reshape(plane, share, LANES)
    mine = jnp.sum(lax.all_to_all(stacked, PLANE, 0, 0), axis=0)
    mine = jnp.broadcast_to(mine[None], (depth, share, LANES))
    return lax.all_to_all(mine, "z", 0, 0)


def gather_sums(shares, parts):
    plane = lax.axis_size(PLANE)
    mine = jnp.sum(shares, axis=0)
    full = lax.all_to_all(jnp.broadcast_to(mine[None], (plane, *mine.shape)), PLANE, 0, 0)
    full = full.reshape(-1, LANES)
    out, start = [], 0
    for part in parts:
        count = part.size // LANES
        out.append(full[start : start + count].reshape(part.shape))
        start += count
    return out


NEAR = ((0, 1), (1, 0), (2, 3), (3, 2))
FAR = ((0, 3), (3, 0), (1, 2), (2, 1))
HIGH, WIDE = 24, 384


def column_of_weights(expand_weight, reduce_weight):
    core, column = lax.axis_index("c"), lax.axis_index("x")
    pair, side = column // 2, column % 2
    thin, units = expand_weight.shape
    part = lax.dynamic_slice(expand_weight, (0, side * (units // 2)), (thin, units // 2))
    row = lax.broadcasted_iota(jnp.int32, (units // 2, 2 * WIDE), 0)
    col = lax.broadcasted_iota(jnp.int32, (units // 2, 2 * WIDE), 1)
    band = col // WIDE * 2 + pair
    at = col % WIDE
    pick = row == at // HIGH * (4 * HIGH) + at % HIGH + band * HIGH
    chosen = jnp.dot(part, pick.astype(jnp.bfloat16), preferred_element_type=jnp.float32)
    both = lax.all_gather(chosen.astype(jnp.bfloat16), "c", axis=0)
    piece = jnp.where(
        lax.axis_index("yh") == 0,
        lax.dynamic_slice(both, (0, 0, core * WIDE), (2, thin, WIDE)).reshape(HIGH, WIDE),
        lax.dynamic_slice(reduce_weight, (pair * HIGH, side * WIDE), (HIGH, WIDE)),
    )
    depth = lax.axis_size("z")
    return lax.all_to_all(jnp.broadcast_to(piece[None], (depth, HIGH, WIDE)), "z", 0, 0)


def sheets_of_weights(column, scaled, masked):
    depth = column.shape[0]
    own = lax.all_to_all(jnp.broadcast_to(column[None], (4, depth, HIGH, WIDE)), ("yh", "yl"), 0, 0)
    own = own.reshape(2, 2 * depth * HIGH, WIDE)
    own, scaled, masked = lax.optimization_barrier((own, scaled, masked))
    own_expand, own_reduce = own[0], own[1]
    near_expand = lax.ppermute(own_expand, "x", NEAR)
    far_reduce = lax.ppermute(own_reduce, "x", FAR)
    near_reduce = lax.ppermute(own_reduce, "x", NEAR)
    far_expand = lax.ppermute(own_expand, "x", FAR)
    across_expand = lax.ppermute(near_expand, "x", FAR)
    across_reduce = lax.ppermute(far_reduce, "x", NEAR)
    scaled = lax.all_gather(scaled, "c", axis=0, tiled=True)
    masked = lax.all_gather(masked, "c", axis=0, tiled=True)
    first = own_expand, near_expand, own_reduce, near_reduce
    second = far_expand, across_expand, far_reduce, across_reduce
    return first, second, scaled, masked


def add_band(band, first_side, cells, scaled_ref, masked_ref, bias_ref, expand, reduce, waits, bias_out, total):
    contract_last = (((1,), (1,)), ((), ()))
    sides = (first_side, 1 - first_side)
    for part in range(2):
        half = pl.ds(pl.multiple_of(sides[part] * WIDE, WIDE), WIDE)
        if waits:
            waits[3 if part else 0].wait()
        hidden = jnp.dot(scaled_ref[cells, :], expand[part][...], preferred_element_type=jnp.float32)
        slope = gelu_slope(hidden + bias_ref[band * 2 + sides[part]])
        back_act = None
        for other in range(2):
            if waits and not part:
                waits[1 + other].wait()
            term = lax.dot_general(
                masked_ref[cells, pl.ds(pl.multiple_of(sides[other] * WIDE, WIDE), WIDE)],
                reduce[other][half, :],
                contract_last,
                preferred_element_type=jnp.float32,
            )
            back_act = term if back_act is None else back_act + term
        back_hidden = (back_act * slope).astype(jnp.bfloat16)
        bias_out[band * 2 + sides[part]] += jnp.sum(back_hidden.astype(jnp.float32), axis=0, keepdims=True)
        total[...] += lax.dot_general(
            back_hidden, expand[part][...], contract_last, preferred_element_type=jnp.float32
        )


def first_body(where_ref, scaled_ref, masked_ref, bias_ref, e0, e1, r0, r1, total_ref, bias_out):
    column, core = where_ref[0], where_ref[1]
    bias_out[...] = jnp.zeros_like(bias_out)
    total_ref[...] = jnp.zeros_like(total_ref)
    add_band(
        2 * core + lax.div(column, 2), lax.rem(column, 2), slice(None), scaled_ref, masked_ref, bias_ref,
        (e0, e1), (r0, r1), (), bias_out, total_ref,
    )


def second_body(
    where_ref, scaled_ref, masked_ref, bias_ref, e0, r0, e1, r1, sum_ref, bias_in,
    mine_ref, other_ref, bias_out, total, expand, reduce, sems,
):
    waits = (
        pltpu.make_async_copy(e0, expand.at[0], sems.at[0]),
        pltpu.make_async_copy(r0, reduce.at[0], sems.at[1]),
        pltpu.make_async_copy(r1, reduce.at[1], sems.at[2]),
        pltpu.make_async_copy(e1, expand.at[1], sems.at[3]),
    )
    for copy in waits:
        copy.start()
    column, core = where_ref[0], where_ref[1]
    cells = mine_ref.shape[0]
    bias_out[...] = bias_in[...]
    total[...] = sum_ref[...]
    add_band(
        2 * core + 1 - lax.div(column, 2), 1 - lax.rem(column, 2), slice(None), scaled_ref, masked_ref, bias_ref,
        (expand.at[0], expand.at[1]), (reduce.at[0], reduce.at[1]), waits, bias_out, total,
    )
    mine_ref[...] = total[pl.ds(pl.multiple_of(core * cells, cells), cells), :]
    other_ref[...] = total[pl.ds(pl.multiple_of((1 - core) * cells, cells), cells), :]


def norm_body(mine_ref, other_ref, normed_ref, inverse_ref, gain_ref, mixed_ref, gain_part_ref):
    gain_part_ref[...] = jnp.zeros_like(gain_part_ref)
    rows = 32

    def finish(step, carry):
        at = pl.ds(pl.multiple_of(step * rows, rows), rows)
        back = (mine_ref[at, :] + other_ref[at, :]).astype(jnp.bfloat16).astype(jnp.float32)
        normed = normed_ref[at, :]
        gain_part_ref[...] += jnp.sum(back * normed, axis=0, keepdims=True)
        back_norm = back * gain_ref[...]
        mixed = inverse_ref[at, :] * (
            back_norm
            - jnp.mean(back_norm, axis=-1, keepdims=True)
            - normed * jnp.mean(back_norm * normed, axis=-1, keepdims=True)
        )
        mixed_ref[at, :] = mixed.astype(jnp.bfloat16)
        return carry

    lax.fori_loop(0, mine_ref.shape[0] // rows, finish, 0)


def pointwise(where, scaled, masked, normed, inverse, gain, bias, first, second):
    cells, channels = normed.shape
    vmem = pl.BlockSpec(memory_space=pltpu.VMEM)
    smem = pl.BlockSpec(memory_space=pltpu.SMEM)
    whole = jax.ShapeDtypeStruct((2 * cells, channels), jnp.float32)
    half = jax.ShapeDtypeStruct((cells, channels), jnp.float32)
    bias_shape = jax.ShapeDtypeStruct(bias.shape, jnp.float32)
    params = pltpu.CompilerParams(vmem_limit_bytes=32 * 1024 * 1024)
    cost = pl.CostEstimate(
        flops=12 * cells * channels * channels, transcendentals=2 * cells * channels, bytes_accessed=20 * 1024 * 1024
    )
    total, bias_part = pl.pallas_call(
        first_body,
        out_shape=(whole, bias_shape),
        in_specs=[smem] + [vmem] * 7,
        out_specs=(vmem, vmem),
        compiler_params=params,
        cost_estimate=cost,
        name="pointwise_first",
    )(where, scaled, masked, bias, *first)
    far_expand, across_expand, far_reduce, across_reduce = second
    mine, other, bias_part = pl.pallas_call(
        second_body,
        out_shape=(half, half, bias_shape),
        in_specs=[smem] + [vmem] * 3 + [pl.BlockSpec(memory_space=pl.ANY)] * 4 + [vmem] * 2,
        out_specs=(vmem, vmem, vmem),
        scratch_shapes=[
            pltpu.VMEM((2 * cells, channels), jnp.float32),
            pltpu.VMEM((2, channels, WIDE), jnp.bfloat16),
            pltpu.VMEM((2, channels, WIDE), jnp.bfloat16),
            pltpu.SemaphoreType.DMA((4,)),
        ],
        compiler_params=params,
        cost_estimate=cost,
        name="pointwise_second",
    )(where, scaled, masked, bias, far_expand, far_reduce, across_expand, across_reduce, total, bias_part)
    other = lax.ppermute(other, "c", ((0, 1), (1, 0)))
    mixed, gain_part = pl.pallas_call(
        norm_body,
        out_shape=(
            jax.ShapeDtypeStruct((cells, channels), jnp.bfloat16),
            jax.ShapeDtypeStruct((1, channels), jnp.float32),
        ),
        in_specs=[vmem] * 5,
        out_specs=(vmem, vmem),
        compiler_params=params,
        name="norm_back",
    )(mine, other, normed, inverse, gain)
    return mixed, gain_part, bias_part


def local(
    ocean_state,
    cotangent,
    depth_kernel,
    norm_gain,
    expand_weight,
    expand_bias,
    reduce_weight,
    tile_slot,
):
    samples, row_count, col_count, channels = ocean_state.shape
    tile_count = tile_slot.shape[0]
    tile_rows = row_count // tile_count
    rim = KS // 2
    weights_column = column_of_weights(expand_weight, reduce_weight)
    rims = exchange_rims(ocean_state, rim)
    padded = join_rims(ocean_state, rims, rim)
    mixed = depthwise(padded, depth_kernel, row_count, col_count)
    centred = mixed - jnp.mean(mixed, axis=-1, keepdims=True)
    inverse = lax.rsqrt(jnp.mean(centred * centred, axis=-1, keepdims=True) + 1e-06)
    normed = centred * inverse
    scaled = (normed * norm_gain).astype(jnp.bfloat16)
    row_mask = jnp.repeat(tile_slot >= 0, tile_rows).astype(jnp.bfloat16)
    masked = cotangent * row_mask[None, :, None, None]
    where = jnp.stack([lax.axis_index("x"), lax.axis_index("c")]).astype(jnp.int32)
    depth = lax.axis_size("z")
    ready = (
        scaled.reshape(-1, channels),
        masked.reshape(-1, channels),
        normed.reshape(-1, channels),
        inverse.reshape(-1, 1),
        norm_gain.reshape(1, channels),
        expand_bias.reshape(2, depth, 4, HIGH).transpose(2, 0, 1, 3).reshape(8, 1, WIDE),
        where,
    )
    scaled, masked, normed, inverse, gain, bias, where = ready
    first, second, scaled, masked = sheets_of_weights(weights_column, scaled, masked)
    back_mixed, gain_part, bias_part = pointwise(
        where, scaled, masked, normed, inverse, gain, bias, first, second
    )
    back_mixed = back_mixed.reshape(samples, row_count, col_count, channels)
    gain_part = gain_part.reshape(channels)
    bias_part = bias_part.reshape(4, 2, depth, HIGH).transpose(1, 2, 0, 3).reshape(-1)
    mixed_float = back_mixed.astype(jnp.float32)
    kernel_rows = []
    for shift_row in range(KS):
        band = padded[:, shift_row : shift_row + row_count, :, :]
        kernel_cols = [
            jnp.sum(
                band[:, :, shift_col : shift_col + col_count, :].astype(jnp.float32) * mixed_float,
                axis=(0, 1, 2),
            )
            for shift_col in range(KS)
        ]
        kernel_rows.append(jnp.stack(kernel_cols))
    kernel_part = jnp.stack(kernel_rows)
    rims = exchange_rims(back_mixed, rim)
    parts = kernel_part, gain_part, bias_part
    shares = sum_shares(parts)
    back_padded = join_rims(back_mixed, rims, rim)
    through = depthwise(back_padded, depth_kernel[::-1, ::-1], row_count, col_count)
    state_grad = (cotangent.astype(jnp.float32) + through).astype(jnp.bfloat16)
    kernel_grad, gain_grad, bias_grad = gather_sums(shares, parts)
    return (state_grad, kernel_grad, gain_grad, bias_grad)


def solution(mesh):
    wide = Mesh(mesh.devices.reshape(2, 4, 2, 16, 2), ("yh", "x", "yl", "z", "c"))
    return jax.shard_map(
        local,
        mesh=wide,
        in_specs=(
            P(DP, TILE, None, None),
            P(DP, TILE, None, None),
            P(),
            P(),
            P(TILE, None),
            P(),
            P(TILE, None),
            P(TILE),
        ),
        out_specs=(P(DP, TILE, None, None), P(), P(), P()),
        check_vma=False,
    )
```
